512 devices in a mesh: virt: 32 (over x, z_lo, core), pair: 16 (over z_hi, y).
Axes of the slice: x: 4, y: 4, z: 16 (z_hi: 4, z_lo: 4; z = z_hi * 4 + z_lo), core: 2. Of those that a mesh axis runs over, the one named last changes fastest.
Arguments:
- amplitudes: float32 [4096, 61440], P('pair', 'virt'), may hold values from -6 to 6
- integrals: float32 [61440, 384], P('virt'), may hold values from -0.09375 to 0.09375
- tile_mask: int32 [640, 4], P('virt'), may hold values from 0 to 1
- mirror_row: int32 [4096], P('pair'), may hold values from 0 to 255, as said below
Outputs:
- residual: float32 [4096, 384], P('pair', 'virt')
The draws below stay inside these ranges and needn't reach their ends.
Inputs may be any that keep to these rules, and one draw needn't show every extreme that they name: For the row at local index l on pair index q, mirror_row is the local index of its mirror pair's row on pair index (q + G / 2) mod G, G = 16; the rows of one device map one to one onto the rows of that device, and the mirror of the mirror is the row itself.
All inputs are finite; a program needn't handle non-finite values.
Results may differ from the reference program's by a relative error of at most 0.000092.
Values sent between devices are 32-bit elements; how exact they have to be, the bound alone decides.
A program may use at most 64 MiB of HBM per device.

```python
import jax
import jax.numpy as jnp
from jax import lax

TILE = 96
KT_DEV = 20
MT = 4
P_DEV = 256
KTILES = 640
K = 61440
M = 384
PAIRS = 4096


def draw_tile_mask(key, part):
    key_live, key_entry, key_level = jax.random.split(key, 3)
    blocks = KTILES // KT_DEV
    level = jax.random.randint(key_level, (blocks, 1), 1, 5)
    live_rows = jax.random.randint(key_live, (blocks, KT_DEV), 0, 4) < level
    live_rows = live_rows.reshape(KTILES, 1).astype(jnp.int32)
    entries = jax.random.randint(key_entry, (KTILES, MT), 0, 2)
    return (live_rows * entries).astype(jnp.int32)


def draw_mirror_row(key, part):
    couples = PAIRS // P_DEV // 2
    subkeys = jax.random.split(key, couples)
    forward = jax.vmap(lambda subkey: jax.random.permutation(subkey, P_DEV))(subkeys).astype(jnp.int32)
    backward = jnp.argsort(forward, axis=1).astype(jnp.int32)
    return jnp.concatenate([forward, backward], axis=0).reshape(PAIRS).astype(jnp.int32)


def spiked(values, stream_key, source, target, parts, factor):
    def block_of(position):
        return (jnp.arange(values.shape[position]) // (values.shape[position] // parts)).reshape((-1,) + (1,) * (values.ndim - 1 - position))

    one_side = jax.random.permutation(stream_key, parts)[block_of(target)]
    far = (block_of(target) + parts // 2) % parts
    return jnp.where((block_of(source) == one_side) | (block_of(source) == far), factor * values, values)


def levels(rng, extent, cuts, smallest, high):
    def one(position, parts):
        heights = jax.random.uniform(jax.random.fold_in(jax.random.fold_in(rng, 6), position), (parts,), jnp.float32, smallest / len(cuts), high / len(cuts))
        return jnp.repeat(jnp.exp(heights), extent[position] // parts).reshape((-1,) + (1,) * (len(extent) - position - 1))

    factor_of = one(*cuts[0])
    for cut in cuts[1:]:
        factor_of = factor_of * one(*cut)
    return factor_of


def gaussian(own_key, extent, deviation, bound, pieces=(), kind=jnp.bfloat16):
    factor_of = levels(own_key, extent, pieces, -0.22, 0.18) if pieces else 1.0
    array = jax.random.normal(own_key, extent, jnp.float32) * deviation * factor_of
    return jnp.minimum(jnp.maximum(array, -bound), bound).astype(kind)


def heavy_noise(own_key, shape, deviation, most, pieces, heavy, held_as=jnp.bfloat16):
    array = deviation * jax.random.normal(own_key, shape, jnp.float32)
    if pieces:
        array = array * levels(own_key, shape, pieces, -0.22, 0.18)
    return jnp.clip(spiked(array, jax.random.fold_in(own_key, 3), *heavy), -most, most).astype(held_as)


def setup_inputs(seed: int = 0) -> dict:
    key_list = jax.random.split(jax.random.key(seed), 5)
    amplitudes = gaussian(key_list[0], (PAIRS, K), 1.0, 6.0, ((0, 16), (1, 32)), jnp.float32)
    integrals = heavy_noise(key_list[1], (K, M), (K // 4) ** -0.5, 0.09375, ((0, 32),), (0, 1, 32, 2.75), jnp.float32)
    tile_mask = draw_tile_mask(jax.random.fold_in(key_list[4], 71), 0)
    mirror_row = draw_mirror_row(jax.random.fold_in(key_list[4], 71), 0)
    return {"amplitudes": amplitudes, "integrals": integrals, "tile_mask": tile_mask, "mirror_row": mirror_row}


def expand_mask(tile_mask):
    expanded = jnp.repeat(tile_mask.astype(jnp.float32), TILE, axis=0)
    return jnp.repeat(expanded, TILE, axis=1)


def reference(amplitudes, integrals, tile_mask, mirror_row):
    masked = integrals * expand_mask(tile_mask)
    ladder = jnp.dot(amplitudes, masked, precision=lax.Precision.HIGHEST, preferred_element_type=jnp.float32)
    turned = jnp.roll(ladder, M // 2, axis=1)
    device_count = PAIRS // P_DEV
    owners = jnp.arange(PAIRS, dtype=jnp.int32) // P_DEV
    partner = (owners + device_count // 2) % device_count
    mirror_global = (partner * P_DEV + mirror_row).astype(jnp.int32)
    return ladder + jnp.take(turned, mirror_global, axis=0)
```

```python
import functools

import jax
import jax.numpy as jnp
from jax import lax
from jax.experimental import pallas as pl
from jax.experimental.pallas import tpu as pltpu
from jax.sharding import PartitionSpec as P

TILE = 96
CHUNKS = ((0, 768), (768, 768), (1536, 384))
F32 = jnp.float32
BF16 = jnp.bfloat16


def split(value):
    high = value.astype(BF16)
    return high, (value - high.astype(F32)).astype(BF16)


def dot(left, right):
    return jnp.dot(left, right, preferred_element_type=F32)


def remote(src, dst, send, recv, virt, pair):
    return pltpu.make_async_remote_copy(
        src_ref=src,
        dst_ref=dst,
        send_sem=send,
        recv_sem=recv,
        device_id={"virt": virt, "pair": pair},
        device_id_type=pl.DeviceIdType.MESH,
    )


def kernel(
    amp_hbm,
    int_hbm,
    mask_ref,
    mirror_ref,
    out_ref,
    amp,
    ints,
    part,
    part_in,
    summed,
    x_in,
    x_sum,
    z_in,
    final,
    own_in,
    mirror_in,
    select,
    load_sem,
    send_sem,
    recv_sem,
):
    virt = lax.axis_index("virt")
    pair = lax.axis_index("pair")
    core = virt % 2
    z = (virt // 2) % 4
    x = virt // 8
    other = 1 - core

    def at(xx, zz, cc):
        return xx * 8 + zz * 2 + cc

    partner = at(x, z, other)
    x_peers = [at((x + d) % 4, z, core) for d in (1, 2, 3)]
    z_peers = [at(x, (z + d) % 4, core) for d in (1, 2, 3)]
    far_pair = (pair + 8) % 16
    far = [at((x + 2) % 4, z, cc) for cc in (0, 1)]

    barrier = pltpu.get_barrier_semaphore()
    for peer in [*x_peers, *z_peers, partner]:
        pl.semaphore_signal(
            barrier, inc=1, device_id={"virt": peer, "pair": pair}, device_id_type=pl.DeviceIdType.MESH
        )
    for peer in far:
        pl.semaphore_signal(
            barrier, inc=1, device_id={"virt": peer, "pair": far_pair}, device_id_type=pl.DeviceIdType.MESH
        )

    loads = []
    for i, (start, size) in enumerate(CHUNKS):
        for j, (src, dst) in enumerate(
            (
                (int_hbm.at[pl.ds(start, size), :], ints.at[pl.ds(start, size), :]),
                (amp_hbm.at[:, pl.ds(start, size)], amp.at[:, pl.ds(start, size)]),
            )
        ):
            copy = pltpu.make_async_copy(src, dst, load_sem.at[2 * i + j])
            copy.start()
            loads.append(copy)

    lane_tile = lax.broadcasted_iota(jnp.int32, (4, 384), 1) // TILE
    row_tile = lax.broadcasted_iota(jnp.int32, (4, 384), 0)
    spread = (lane_tile == row_tile).astype(F32)
    mask = lax.dot_general(
        mask_ref[...].astype(F32), spread, (((0,), (0,)), ((), ())), preferred_element_type=F32
    )
    rows = lax.broadcasted_iota(jnp.int32, (256, 256), 0)
    select[...] = (rows == mirror_ref[...]).astype(F32).astype(BF16)

    total = jnp.zeros((256, 384), F32)
    for i, (start, size) in enumerate(CHUNKS):
        loads[2 * i].wait()
        loads[2 * i + 1].wait()
        tiles = []
        for t in range(start // TILE, (start + size) // TILE):
            tiles.append(ints[t * TILE : (t + 1) * TILE, :] * mask[t : t + 1, :])
        b_high, b_low = split(jnp.concatenate(tiles, axis=0))
        a_high, a_low = split(amp[:, start : start + size])
        total += dot(a_high, b_high) + dot(a_high, b_low) + dot(a_low, b_high)
    part[0] = total[:128].T
    part[1] = total[128:].T

    pl.semaphore_wait(barrier, 9)

    sends = []

    def send(slot, src, dst, virt_to, pair_to):
        copy = remote(src, dst, send_sem.at[slot], recv_sem.at[slot], virt_to, pair_to)
        copy.start()
        sends.append(copy)

    send(0, part.at[other], part_in, partner, pair)
    sends[0].wait_recv()
    summed[...] = part[core] + part_in[...]

    for d in (1, 2, 3):
        block = pl.ds(((x + d) % 4) * 96, 96)
        send(d, summed.at[block], x_in.at[d - 1], x_peers[d - 1], pair)
    for d in (1, 2, 3):
        sends[d].wait_recv()
    x_sum[...] = summed[pl.ds(x * 96, 96), :] + x_in[0] + x_in[1] + x_in[2]

    for d in (1, 2, 3):
        block = pl.ds(((z + d) % 4) * 24, 24)
        send(3 + d, x_sum.at[block], z_in.at[d - 1], z_peers[d - 1], pair)
    for d in (1, 2, 3):
        sends[3 + d].wait_recv()
    final[...] = x_sum[pl.ds(z * 24, 24), :] + z_in[0] + z_in[1] + z_in[2]

    for cc in (0, 1):
        copy = remote(
            final.at[pl.ds(8 * cc, 16)],
            mirror_in.at[core],
            send_sem.at[7 + cc],
            recv_sem.at[7 + core],
            far[cc],
            far_pair,
        )
        copy.start()
        sends.append(copy)
    send(9, final.at[pl.ds(8 * other, 16)], own_in, partner, pair)

    def pick(value):
        return jnp.where(core == 0, value[0:12], value[4:16])

    sends[9].wait_recv()
    mine = final[...]
    mine = jnp.where(core == 0, mine[0:12], mine[12:24])
    theirs = pick(own_in[...])
    low_half = jnp.where(core == 0, mine, theirs)
    high_half = jnp.where(core == 0, theirs, mine)
    own = jnp.concatenate([low_half, high_half], axis=1)

    for half in (0, 1):
        pltpu.make_async_copy(mirror_in.at[half], mirror_in.at[half], recv_sem.at[7 + half]).wait()
    turned = jnp.concatenate([pick(mirror_in[0]), pick(mirror_in[1])], axis=1)
    first, rest = turned.astype(BF16), turned
    rest = turned - first.astype(F32)
    second = rest.astype(BF16)
    third = (rest - second.astype(F32)).astype(BF16)
    matrix = select[...]
    out_ref[...] = own + (dot(first, matrix) + dot(second, matrix) + dot(third, matrix))

    for copy in sends:
        copy.wait_send()


def shards(amplitudes, integrals, tile_mask, mirror_row):
    any_spec = pl.BlockSpec(memory_space=pl.ANY)
    vmem_spec = pl.BlockSpec(memory_space=pltpu.VMEM)
    result = pl.pallas_call(
        kernel,
        out_shape=jax.ShapeDtypeStruct((12, 256), F32),
        in_specs=[any_spec, any_spec, vmem_spec, vmem_spec],
        out_specs=vmem_spec,
        scratch_shapes=[
            pltpu.VMEM((256, 1920), F32),
            pltpu.VMEM((1920, 384), F32),
            pltpu.VMEM((2, 384, 128), F32),
            pltpu.VMEM((384, 128), F32),
            pltpu.VMEM((384, 128), F32),
            pltpu.VMEM((3, 96, 128), F32),
            pltpu.VMEM((96, 128), F32),
            pltpu.VMEM((3, 24, 128), F32),
            pltpu.VMEM((24, 128), F32),
            pltpu.VMEM((16, 128), F32),
            pltpu.VMEM((2, 16, 128), F32),
            pltpu.VMEM((256, 256), BF16),
            pltpu.SemaphoreType.DMA((6,)),
            pltpu.SemaphoreType.DMA((10,)),
            pltpu.SemaphoreType.DMA((10,)),
        ],
        compiler_params=pltpu.CompilerParams(collective_id=0, has_side_effects=True),
        name="ladder",
    )(amplitudes, integrals, tile_mask.T, mirror_row.reshape(1, 256))
    return result.T


def solution(mesh):
    in_specs = (P("pair", "virt"), P("virt", None), P("virt", None), P("pair"))
    out_specs = P("pair", "virt")
    return jax.shard_map(shards, mesh=mesh, in_specs=in_specs, out_specs=out_specs, check_vma=False)
```

```python
import jax
import jax.numpy as jnp
from jax import lax
from jax.experimental import pallas as pl
from jax.experimental.pallas import tpu as pltpu
from jax.sharding import PartitionSpec as P

TILE = 96
CHUNKS = ((0, 768), (768, 768), (1536, 384))
F32 = jnp.float32
BF16 = jnp.bfloat16
MESH = pl.DeviceIdType.MESH


def split(value):
    high = value.astype(BF16)
    return high, (value - high.astype(F32)).astype(BF16)


def dot(left, right):
    return jnp.dot(left, right, preferred_element_type=F32)


def unpack(block):
    return jnp.concatenate([block[0:12], block[12:24]], axis=1)


def kernel(
    amp_hbm,
    int_hbm,
    mask_hbm,
    mirror_hbm,
    out_ref,
    amp,
    ints,
    mask_in,
    mirror_row,
    part,
    part_in,
    summed,
    far_x_in,
    far_x_sum,
    far_in,
    own_x_in,
    own_x_sum,
    own_z_in,
    select,
    load_sem,
    send_sem,
    recv_sem,
):
    loads = [pltpu.make_async_copy(mask_hbm, mask_in, load_sem.at[0])]
    for i, (start, size) in enumerate(CHUNKS):
        loads.append(
            pltpu.make_async_copy(
                int_hbm.at[pl.ds(start, size), :], ints.at[pl.ds(start, size), :], load_sem.at[2 * i + 1]
            )
        )
        loads.append(
            pltpu.make_async_copy(
                amp_hbm.at[:, pl.ds(start, size)], amp.at[:, pl.ds(start, size)], load_sem.at[2 * i + 2]
            )
        )
    loads.append(pltpu.make_async_copy(mirror_hbm, mirror_row, load_sem.at[7]))
    for load in loads:
        load.start()

    virt = lax.axis_index("virt")
    pair = lax.axis_index("pair")
    core = virt % 2
    z = (virt // 2) % 4
    x = virt // 8
    other = 1 - core
    far_pair = (pair + 8) % 16

    def at(xx, zz, cc):
        return xx * 8 + zz * 2 + cc

    partner = at(x, z, other)
    x_peers = [at((x + d) % 4, z, core) for d in (1, 2, 3)]
    z_peers = [at(x, (z + d) % 4, core) for d in (1, 2, 3)]
    far_peers = [at(x, (z + d) % 4, core) for d in (0, 1, 2, 3)]

    barrier = pltpu.get_barrier_semaphore()
    for peer in far_peers:
        pl.semaphore_signal(barrier, inc=1, device_id={"virt": peer, "pair": far_pair}, device_id_type=MESH)
    for peer in [*x_peers, *z_peers, partner]:
        pl.semaphore_signal(barrier, inc=1, device_id={"virt": peer, "pair": pair}, device_id_type=MESH)

    lane_tile = lax.broadcasted_iota(jnp.int32, (4, 384), 1) // TILE
    row_tile = lax.broadcasted_iota(jnp.int32, (4, 384), 0)
    spread = (lane_tile == row_tile).astype(F32)
    loads[0].wait()
    mask = lax.dot_general(
        mask_in[...].astype(F32), spread, (((0,), (0,)), ((), ())), preferred_element_type=F32
    )

    total = jnp.zeros((256, 384), F32)
    for i, (start, size) in enumerate(CHUNKS):
        loads[2 * i + 1].wait()
        loads[2 * i + 2].wait()
        tiles = []
        for t in range(start // TILE, (start + size) // TILE):
            tiles.append(ints[t * TILE : (t + 1) * TILE, :] * mask[t : t + 1, :])
        b_high, b_low = split(jnp.concatenate(tiles, axis=0))
        a_high, a_low = split(amp[:, start : start + size])
        total += dot(a_high, b_high) + dot(a_high, b_low) + dot(a_low, b_high)
    left = total[:128].T
    right = total[128:].T
    for cc in (0, 1):
        for b in range(16):
            first = 24 * b + 12 * cc
            part[cc, b] = jnp.concatenate([left[first : first + 12], right[first : first + 12]], axis=0)

    pl.semaphore_wait(barrier, 11)

    sends = []

    def send(slot, src, dst, virt_to, pair_to):
        copy = pltpu.make_async_remote_copy(
            src_ref=src,
            dst_ref=dst,
            send_sem=send_sem.at[slot],
            recv_sem=recv_sem.at[slot],
            device_id={"virt": virt_to, "pair": pair_to},
            device_id_type=MESH,
        )
        copy.start()
        sends.append(copy)
        return copy

    order = (2, 1, 3, 0)
    halves = []
    for i, d in enumerate(order):
        block = pl.ds(((x + 2 + d) % 4) * 4, 4)
        halves.append(send(i, part.at[other, block], part_in.at[i], partner, pair))

    loads[7].wait()
    rows = lax.broadcasted_iota(jnp.int32, (256, 256), 0)
    select[...] = (rows == mirror_row[...]).astype(F32).astype(BF16)

    arrivals = []
    for i, d in enumerate(order):
        block = pl.ds(((x + 2 + d) % 4) * 4, 4)
        halves[i].wait_recv()
        summed[block] = part[core, block] + part_in[i]
        if d:
            arrivals.append(send(3 + d, summed.at[block], far_x_in.at[d - 1], x_peers[d - 1], pair))
    for copy in arrivals:
        copy.wait_recv()
    far_x_sum[...] = summed[pl.ds(((x + 2) % 4) * 4, 4)] + far_x_in[0] + far_x_in[1] + far_x_in[2]

    far = []
    for d in (0, 1, 3, 2):
        copy = pltpu.make_async_remote_copy(
            src_ref=far_x_sum.at[(z + d) % 4],
            dst_ref=far_in.at[d],
            send_sem=send_sem.at[7 + d],
            recv_sem=recv_sem.at[7 + d],
            device_id={"virt": far_peers[d], "pair": far_pair},
            device_id_type=MESH,
        )
        copy.start()
        sends.append(copy)
        far.append(copy)

    arrivals = []
    for d in (2, 1, 3):
        block = pl.ds(((x + d) % 4) * 4, 4)
        arrivals.append(send(10 + d, summed.at[block], own_x_in.at[d - 1], x_peers[d - 1], pair))
    for copy in arrivals:
        copy.wait_recv()
    own_x_sum[...] = summed[pl.ds(x * 4, 4)] + own_x_in[0] + own_x_in[1] + own_x_in[2]
    arrivals = []
    for d in (1, 2, 3):
        arrivals.append(send(13 + d, own_x_sum.at[(z + d) % 4], own_z_in.at[d - 1], z_peers[d - 1], pair))
    for copy in arrivals:
        copy.wait_recv()
    own = unpack(own_x_sum[z] + own_z_in[0] + own_z_in[1] + own_z_in[2])

    for copy in far:
        copy.wait_recv()
    turned = unpack(far_in[0] + far_in[1] + far_in[2] + far_in[3])
    first = turned.astype(BF16)
    rest = turned - first.astype(F32)
    second, third = split(rest)
    matrix = select[...]
    out_ref[...] = own + (dot(first, matrix) + dot(second, matrix) + dot(third, matrix))

    for copy in sends:
        copy.wait_send()


def shards(amplitudes, integrals, tile_mask, mirror_row):
    any_spec = pl.BlockSpec(memory_space=pl.ANY)
    result = pl.pallas_call(
        kernel,
        out_shape=jax.ShapeDtypeStruct((12, 256), F32),
        in_specs=[any_spec] * 4,
        out_specs=pl.BlockSpec(memory_space=pltpu.VMEM),
        scratch_shapes=[
            pltpu.VMEM((256, 1920), F32),
            pltpu.VMEM((1920, 384), F32),
            pltpu.VMEM((4, 20), jnp.int32),
            pltpu.VMEM((1, 256), jnp.int32),
            pltpu.VMEM((2, 16, 24, 128), F32),
            pltpu.VMEM((4, 4, 24, 128), F32),
            pltpu.VMEM((16, 24, 128), F32),
            pltpu.VMEM((3, 4, 24, 128), F32),
            pltpu.VMEM((4, 24, 128), F32),
            pltpu.VMEM((4, 24, 128), F32),
            pltpu.VMEM((3, 4, 24, 128), F32),
            pltpu.VMEM((4, 24, 128), F32),
            pltpu.VMEM((3, 24, 128), F32),
            pltpu.VMEM((256, 256), BF16),
            pltpu.SemaphoreType.DMA((8,)),
            pltpu.SemaphoreType.DMA((17,)),
            pltpu.SemaphoreType.DMA((17,)),
        ],
        compiler_params=pltpu.CompilerParams(collective_id=0, has_side_effects=True),
        name="ladder",
    )(amplitudes, integrals, tile_mask.T, mirror_row.reshape(1, 256))
    return result.T


def solution(mesh):
    in_specs = (P("pair", "virt"), P("virt", None), P("virt", None), P("pair"))
    out_specs = P("pair", "virt")
    return jax.shard_map(shards, mesh=mesh, in_specs=in_specs, out_specs=out_specs, check_vma=False)
```

```python
import jax
import jax.numpy as jnp
from jax import lax
from jax.experimental import pallas as pl
from jax.experimental.pallas import tpu as pltpu
from jax.sharding import PartitionSpec as P

TILE = 96
CHUNKS = ((0, 768), (768, 768), (1536, 384))
F32 = jnp.float32
BF16 = jnp.bfloat16
MESH = pl.DeviceIdType.MESH


def split(value):
    high = value.astype(BF16)
    return high, (value - high.astype(F32)).astype(BF16)


def dot(left, right):
    return jnp.dot(left, right, preferred_element_type=F32)


def unpack(block):
    return jnp.concatenate([block[0:12], block[12:24]], axis=1)


def kernel(
    amp_hbm,
    int_hbm,
    mask_hbm,
    mirror_hbm,
    out_ref,
    amp,
    ints,
    mask_in,
    mirror_row,
    part,
    part_in,
    summed,
    far_x_in,
    far_x_sum,
    far_in,
    own_x_in,
    own_x_sum,
    own_z_in,
    select,
    load_sem,
    send_sem,
    recv_sem,
    next_sem,
    far_sem,
):
    loads = [pltpu.make_async_copy(mask_hbm, mask_in, load_sem.at[0])]
    for i, (start, size) in enumerate(CHUNKS):
        loads.append(
            pltpu.make_async_copy(
                int_hbm.at[pl.ds(start, size), :], ints.at[pl.ds(start, size), :], load_sem.at[2 * i + 1]
            )
        )
        loads.append(
            pltpu.make_async_copy(
                amp_hbm.at[:, pl.ds(start, size)], amp.at[:, pl.ds(start, size)], load_sem.at[2 * i + 2]
            )
        )
    loads.append(pltpu.make_async_copy(mirror_hbm, mirror_row, load_sem.at[7]))
    for load in loads:
        load.start()

    virt = lax.axis_index("virt")
    pair = lax.axis_index("pair")
    core = virt % 2
    z = (virt // 2) % 4
    x = virt // 8
    other = 1 - core
    far_pair = (pair + 8) % 16

    def at(xx, zz, cc):
        return xx * 8 + zz * 2 + cc

    partner = at(x, z, other)
    x_peers = [at((x + d) % 4, z, core) for d in (1, 2, 3)]
    z_peers = [at(x, (z + d) % 4, core) for d in (1, 2, 3)]
    far_peers = [at(x, (z + d) % 4, core) for d in (0, 1, 2, 3)]

    barrier = pltpu.get_barrier_semaphore()

    def signal(semaphore, virt_to, pair_to):
        pl.semaphore_signal(semaphore, inc=1, device_id={"virt": virt_to, "pair": pair_to}, device_id_type=MESH)

    next_pair = (pair + 4) % 16
    last_pair = (pair + 12) % 16
    signal(barrier, virt, next_pair)
    signal(barrier, virt, last_pair)
    for peer in [*z_peers, *x_peers, partner]:
        signal(barrier, peer, pair)

    lane_tile = lax.broadcasted_iota(jnp.int32, (4, 384), 1) // TILE
    row_tile = lax.broadcasted_iota(jnp.int32, (4, 384), 0)
    spread = (lane_tile == row_tile).astype(F32)
    loads[0].wait()
    mask = lax.dot_general(
        mask_in[...].astype(F32), spread, (((0,), (0,)), ((), ())), preferred_element_type=F32
    )

    total = jnp.zeros((256, 384), F32)
    for i, (start, size) in enumerate(CHUNKS):
        loads[2 * i + 1].wait()
        loads[2 * i + 2].wait()
        if i == len(CHUNKS) - 1:
            pl.semaphore_wait(barrier, 9)
            signal(next_sem, virt, last_pair)
        tiles = []
        for t in range(start // TILE, (start + size) // TILE):
            tiles.append(ints[t * TILE : (t + 1) * TILE, :] * mask[t : t + 1, :])
        b_high, b_low = split(jnp.concatenate(tiles, axis=0))
        a_high, a_low = split(amp[:, start : start + size])
        total += dot(a_high, b_high) + dot(a_high, b_low) + dot(a_low, b_high)
    left = total[:128].T
    right = total[128:].T
    for zb in range(4):
        for xb in range(4):
            for cc in (0, 1):
                first = 24 * (4 * xb + zb) + 12 * cc
                part[cc, zb, xb] = jnp.concatenate(
                    [left[first : first + 12], right[first : first + 12]], axis=0
                )

    sends = []

    def send(slot, src, dst, virt_to, pair_to):
        copy = pltpu.make_async_remote_copy(
            src_ref=src,
            dst_ref=dst,
            send_sem=send_sem.at[slot],
            recv_sem=recv_sem.at[slot],
            device_id={"virt": virt_to, "pair": pair_to},
            device_id_type=MESH,
        )
        copy.start()
        sends.append(copy)
        return copy

    order = (0, 1, 3, 2)
    halves = []
    for i, d in enumerate(order):
        block = (z + d) % 4
        halves.append(send(i, part.at[other, block], part_in.at[i], partner, pair))

    loads[7].wait()
    rows = lax.broadcasted_iota(jnp.int32, (256, 256), 0)
    select[...] = (rows == mirror_row[...]).astype(F32).astype(BF16)

    arrivals = []
    for i, d in enumerate(order):
        block = (z + d) % 4
        halves[i].wait_recv()
        summed[block] = part[core, block] + part_in[i]
        for dx in (2, 1, 3):
            column = (x + 2 + dx) % 4
            arrivals.append(
                send(
                    4 + 3 * i + dx - 1,
                    summed.at[block, column],
                    far_x_in.at[dx - 1, i],
                    x_peers[dx - 1],
                    pair,
                )
            )
    pl.semaphore_wait(next_sem, 1)
    for peer in z_peers:
        signal(far_sem, peer, pair)
    far = []
    for i, d in enumerate(order):
        if i == 1:
            pl.semaphore_wait(far_sem, 3)
        for copy in arrivals[3 * i : 3 * i + 3]:
            copy.wait_recv()
        kept = summed[(z + d) % 4, (x + 2) % 4]
        far_x_sum[i] = kept + far_x_in[0, i] + far_x_in[1, i] + far_x_in[2, i]
        far.append(send(16 + i, far_x_sum.at[i], far_in.at[i], far_peers[d], far_pair))

    own_order = (2, 1, 3, 0)
    arrivals = []
    for i, d in enumerate(own_order):
        for dx in (2, 1, 3):
            column = (x + dx) % 4
            arrivals.append(
                send(
                    20 + 3 * i + dx - 1,
                    summed.at[(z + d) % 4, column],
                    own_x_in.at[dx - 1, i],
                    x_peers[dx - 1],
                    pair,
                )
            )
    own_z = []
    for i, d in enumerate(own_order):
        for copy in arrivals[3 * i : 3 * i + 3]:
            copy.wait_recv()
        kept = summed[(z + d) % 4, x] + own_x_in[0, i] + own_x_in[1, i] + own_x_in[2, i]
        if d:
            own_x_sum[i] = kept
            own_z.append(send(32 + i, own_x_sum.at[i], own_z_in.at[i], z_peers[d - 1], pair))
    for copy in own_z:
        copy.wait_recv()
    own = unpack(kept + own_z_in[0] + own_z_in[1] + own_z_in[2])

    for copy in far:
        copy.wait_recv()
    turned = unpack(far_in[0] + far_in[1] + far_in[2] + far_in[3])
    first = turned.astype(BF16)
    rest = turned - first.astype(F32)
    second, third = split(rest)
    matrix = select[...]
    out_ref[...] = own + (dot(first, matrix) + dot(second, matrix) + dot(third, matrix))

    for copy in sends:
        copy.wait_send()


def shards(amplitudes, integrals, tile_mask, mirror_row):
    any_spec = pl.BlockSpec(memory_space=pl.ANY)
    result = pl.pallas_call(
        kernel,
        out_shape=pltpu.VMEM((12, 256), F32),
        in_specs=[any_spec] * 4,
        out_specs=pl.BlockSpec(memory_space=pltpu.VMEM),
        scratch_shapes=[
            pltpu.VMEM((256, 1920), F32),
            pltpu.VMEM((1920, 384), F32),
            pltpu.VMEM((4, 20), jnp.int32),
            pltpu.VMEM((1, 256), jnp.int32),
            pltpu.VMEM((2, 4, 4, 24, 128), F32),
            pltpu.VMEM((4, 4, 24, 128), F32),
            pltpu.VMEM((4, 4, 24, 128), F32),
            pltpu.VMEM((3, 4, 24, 128), F32),
            pltpu.VMEM((4, 24, 128), F32),
            pltpu.VMEM((4, 24, 128), F32),
            pltpu.VMEM((3, 4, 24, 128), F32),
            pltpu.VMEM((3, 24, 128), F32),
            pltpu.VMEM((3, 24, 128), F32),
            pltpu.VMEM((256, 256), BF16),
            pltpu.SemaphoreType.DMA((8,)),
            pltpu.SemaphoreType.DMA((35,)),
            pltpu.SemaphoreType.DMA((35,)),
            pltpu.SemaphoreType.REGULAR,
            pltpu.SemaphoreType.REGULAR,
        ],
        compiler_params=pltpu.CompilerParams(collective_id=0, has_side_effects=True),
        name="ladder",
    )(amplitudes, integrals, tile_mask.T, mirror_row.reshape(1, 256))
    return result.T


def solution(mesh):
    in_specs = (P("pair", "virt"), P("virt", None), P("virt", None), P("pair"))
    out_specs = P("pair", "virt")
    return jax.shard_map(shards, mesh=mesh, in_specs=in_specs, out_specs=out_specs, check_vma=False)
```

```python
import jax
import jax.numpy as jnp
from jax import lax
from jax.experimental import pallas as pl
from jax.experimental.pallas import tpu as pltpu
from jax.sharding import PartitionSpec as P

TILE = 96
CHUNKS = ((0, 768), (768, 768), (1536, 384))
F32 = jnp.float32
BF16 = jnp.bfloat16
MESH = pl.DeviceIdType.MESH


def split(value):
    high = value.astype(BF16)
    return high, (value - high.astype(F32)).astype(BF16)


def dot(left, right):
    return jnp.dot(left, right, preferred_element_type=F32)


def unpack(block):
    return jnp.concatenate([block[0:12], block[12:24]], axis=1)


def kernel(
    amp_hbm,
    int_hbm,
    mask_hbm,
    mirror_hbm,
    out_ref,
    amp,
    ints,
    mask_in,
    mirror_row,
    part,
    part_in,
    summed,
    far_x_in,
    far_x_sum,
    far_in,
    own_x_in,
    own_x_sum,
    own_z_in,
    select,
    load_sem,
    send_sem,
    recv_sem,
    ready,
):
    loads = [pltpu.make_async_copy(mask_hbm, mask_in, load_sem.at[0])]
    for i, (start, size) in enumerate(CHUNKS):
        loads.append(
            pltpu.make_async_copy(
                int_hbm.at[pl.ds(start, size), :], ints.at[pl.ds(start, size), :], load_sem.at[2 * i + 1]
            )
        )
        loads.append(
            pltpu.make_async_copy(
                amp_hbm.at[:, pl.ds(start, size)], amp.at[:, pl.ds(start, size)], load_sem.at[2 * i + 2]
            )
        )
    loads.append(pltpu.make_async_copy(mirror_hbm, mirror_row, load_sem.at[7]))
    for load in loads:
        load.start()

    virt = lax.axis_index("virt")
    pair = lax.axis_index("pair")
    core = virt % 2
    z = (virt // 2) % 4
    x = virt // 8
    other = 1 - core
    far_pair = (pair + 8) % 16

    def at(xx, zz, cc):
        return xx * 8 + zz * 2 + cc

    partner = at(x, z, other)
    x_peers = [at((x + d) % 4, z, core) for d in (1, 2, 3)]
    z_peers = [at(x, (z + d) % 4, core) for d in (1, 2, 3)]
    far_peers = [at(x, d, core) for d in (0, 1, 2, 3)]

    late = pair // 8
    barrier = pltpu.get_barrier_semaphore()

    def signal(semaphore, virt_to, pair_to):
        pl.semaphore_signal(semaphore, inc=1, device_id={"virt": virt_to, "pair": pair_to}, device_id_type=MESH)

    @pl.when(late == 0)
    def _():
        for peer in far_peers:
            signal(barrier, peer, far_pair)

    for peer in [*x_peers, *z_peers, partner]:
        signal(barrier, peer, pair)

    lane_tile = lax.broadcasted_iota(jnp.int32, (4, 384), 1) // TILE
    row_tile = lax.broadcasted_iota(jnp.int32, (4, 384), 0)
    spread = (lane_tile == row_tile).astype(F32)
    loads[0].wait()
    mask = lax.dot_general(
        mask_in[...].astype(F32), spread, (((0,), (0,)), ((), ())), preferred_element_type=F32
    )

    total = jnp.zeros((256, 384), F32)
    for i, (start, size) in enumerate(CHUNKS):
        loads[2 * i + 1].wait()
        loads[2 * i + 2].wait()
        if i == len(CHUNKS) - 1:
            pl.semaphore_wait(barrier, 7 + 4 * late)

            @pl.when(late == 1)
            def _():
                for peer in far_peers:
                    signal(ready, peer, far_pair)

        tiles = []
        for t in range(start // TILE, (start + size) // TILE):
            tiles.append(ints[t * TILE : (t + 1) * TILE, :] * mask[t : t + 1, :])
        b_high, b_low = split(jnp.concatenate(tiles, axis=0))
        a_high, a_low = split(amp[:, start : start + size])
        total += dot(a_high, b_high) + dot(a_high, b_low) + dot(a_low, b_high)
    left = total[:128].T
    right = total[128:].T
    for zb in range(4):
        for xb in range(4):
            for cc in (0, 1):
                first = 24 * (4 * xb + zb) + 12 * cc
                part[cc, zb, xb] = jnp.concatenate(
                    [left[first : first + 12], right[first : first + 12]], axis=0
                )

    sends = []

    def send(slot, src, dst, virt_to, pair_to):
        copy = pltpu.make_async_remote_copy(
            src_ref=src,
            dst_ref=dst,
            send_sem=send_sem.at[slot],
            recv_sem=recv_sem.at[slot],
            device_id={"virt": virt_to, "pair": pair_to},
            device_id_type=MESH,
        )
        copy.start()
        sends.append(copy)
        return copy

    order = (0, 1, 2, 3)
    halves = []
    for i, d in enumerate(order):
        block = d
        halves.append(send(i, part.at[other, block], part_in.at[i], partner, pair))

    loads[7].wait()
    rows = lax.broadcasted_iota(jnp.int32, (256, 256), 0)
    select[...] = (rows == mirror_row[...]).astype(F32).astype(BF16)

    arrivals = []
    for i, d in enumerate(order):
        block = d
        halves[i].wait_recv()
        summed[block] = part[core, block] + part_in[i]
        for dx in (2, 1, 3):
            column = (x + 2 + dx) % 4
            arrivals.append(
                send(
                    4 + 3 * i + dx - 1,
                    summed.at[block, column],
                    far_x_in.at[dx - 1, i],
                    x_peers[dx - 1],
                    pair,
                )
            )
    far = []
    for i, d in enumerate(order):
        far.append(
            pltpu.make_async_remote_copy(
                src_ref=far_x_sum.at[i],
                dst_ref=far_in.at[z],
                send_sem=send_sem.at[16 + i],
                recv_sem=recv_sem.at[16 + z],
                device_id={"virt": far_peers[d], "pair": far_pair},
                device_id_type=MESH,
            )
        )
    for i, d in enumerate(order):
        for copy in arrivals[3 * i : 3 * i + 3]:
            copy.wait_recv()
        kept = summed[d, (x + 2) % 4]
        far_x_sum[i] = kept + far_x_in[0, i] + far_x_in[1, i] + far_x_in[2, i]

        @pl.when(late == 1)
        def _(copy=far[i]):
            copy.start()

    own_order = (2, 1, 3, 0)
    arrivals = []
    for i, d in enumerate(own_order):
        for dx in (2, 1, 3):
            column = (x + dx) % 4
            arrivals.append(
                send(
                    20 + 3 * i + dx - 1,
                    summed.at[(z + d) % 4, column],
                    own_x_in.at[dx - 1, i],
                    x_peers[dx - 1],
                    pair,
                )
            )
    own_z = []
    for i, d in enumerate(own_order):
        for copy in arrivals[3 * i : 3 * i + 3]:
            copy.wait_recv()
        kept = summed[(z + d) % 4, x] + own_x_in[0, i] + own_x_in[1, i] + own_x_in[2, i]
        if d:
            own_x_sum[i] = kept
            own_z.append(send(32 + i, own_x_sum.at[i], own_z_in.at[i], z_peers[d - 1], pair))
    @pl.when(late == 0)
    def _():
        pl.semaphore_wait(ready, 4)
        for copy in far:
            copy.start()

    for copy in own_z:
        copy.wait_recv()
    own = unpack(kept + own_z_in[0] + own_z_in[1] + own_z_in[2])

    for slot in range(4):
        pltpu.make_async_copy(far_in.at[slot], far_in.at[slot], recv_sem.at[16 + slot]).wait()
    turned = unpack(far_in[0] + far_in[1] + far_in[2] + far_in[3])
    first = turned.astype(BF16)
    rest = turned - first.astype(F32)
    second, third = split(rest)
    matrix = select[...]
    out_ref[...] = own + (dot(first, matrix) + dot(second, matrix) + dot(third, matrix))

    for copy in [*sends, *far]:
        copy.wait_send()


def shards(amplitudes, integrals, tile_mask, mirror_row):
    any_spec = pl.BlockSpec(memory_space=pl.ANY)
    result = pl.pallas_call(
        kernel,
        out_shape=pltpu.VMEM((12, 256), F32),
        in_specs=[any_spec] * 4,
        out_specs=pl.BlockSpec(memory_space=pltpu.VMEM),
        scratch_shapes=[
            pltpu.VMEM((256, 1920), F32),
            pltpu.VMEM((1920, 384), F32),
            pltpu.VMEM((4, 20), jnp.int32),
            pltpu.VMEM((1, 256), jnp.int32),
            pltpu.VMEM((2, 4, 4, 24, 128), F32),
            pltpu.VMEM((4, 4, 24, 128), F32),
            pltpu.VMEM((4, 4, 24, 128), F32),
            pltpu.VMEM((3, 4, 24, 128), F32),
            pltpu.VMEM((4, 24, 128), F32),
            pltpu.VMEM((4, 24, 128), F32),
            pltpu.VMEM((3, 4, 24, 128), F32),
            pltpu.VMEM((3, 24, 128), F32),
            pltpu.VMEM((3, 24, 128), F32),
            pltpu.VMEM((256, 256), BF16),
            pltpu.SemaphoreType.DMA((8,)),
            pltpu.SemaphoreType.DMA((35,)),
            pltpu.SemaphoreType.DMA((35,)),
            pltpu.SemaphoreType.REGULAR,
        ],
        compiler_params=pltpu.CompilerParams(collective_id=0, has_side_effects=True),
        name="ladder",
    )(amplitudes, integrals, tile_mask.T, mirror_row.reshape(1, 256))
    return result.T


def solution(mesh):
    in_specs = (P("pair", "virt"), P("virt", None), P("virt", None), P("pair"))
    out_specs = P("pair", "virt")
    return jax.shard_map(shards, mesh=mesh, in_specs=in_specs, out_specs=out_specs, check_vma=False)
```

```python
import jax
import jax.numpy as jnp
from jax import lax
from jax.experimental import pallas as pl
from jax.experimental.pallas import tpu as pltpu
from jax.sharding import PartitionSpec as P

TILE = 96
CHUNKS = ((0, 768), (768, 768), (1536, 384))
F32 = jnp.float32
BF16 = jnp.bfloat16
MESH = pl.DeviceIdType.MESH


def split(value):
    high = value.astype(BF16)
    return high, (value - high.astype(F32)).astype(BF16)


def dot(left, right):
    return jnp.dot(left, right, preferred_element_type=F32)


def unpack(block):
    return jnp.concatenate([block[0:12], block[12:24]], axis=1)


def kernel(
    amp_hbm,
    int_hbm,
    mask_hbm,
    mirror_hbm,
    out_ref,
    amp,
    ints,
    mask_in,
    mirror_row,
    part,
    part_in,
    summed,
    far_x_in,
    cross_in,
    far_x_sum,
    far_in,
    own_x_in,
    own_x_sum,
    own_z_in,
    select,
    load_sem,
    send_sem,
    recv_sem,
    ready,
):
    loads = [pltpu.make_async_copy(mask_hbm, mask_in, load_sem.at[0])]
    for i, (start, size) in enumerate(CHUNKS):
        loads.append(
            pltpu.make_async_copy(
                int_hbm.at[pl.ds(start, size), :], ints.at[pl.ds(start, size), :], load_sem.at[2 * i + 1]
            )
        )
        loads.append(
            pltpu.make_async_copy(
                amp_hbm.at[:, pl.ds(start, size)], amp.at[:, pl.ds(start, size)], load_sem.at[2 * i + 2]
            )
        )
    loads.append(pltpu.make_async_copy(mirror_hbm, mirror_row, load_sem.at[7]))
    for load in loads:
        load.start()

    virt = lax.axis_index("virt")
    pair = lax.axis_index("pair")
    core = virt % 2
    z = (virt // 2) % 4
    x = virt // 8
    other = 1 - core
    far_pair = (pair + 8) % 16

    def at(xx, zz, cc):
        return xx * 8 + zz * 2 + cc

    partner = at(x, z, other)
    x_peers = [at((x + d) % 4, z, core) for d in (1, 2, 3)]
    cross_peers = [at((x + d) % 4, z, other) for d in (1, 2, 3)]
    z_peers = [at(x, (z + d) % 4, core) for d in (1, 2, 3)]
    far_peers = [at(x, d, core) for d in (0, 1, 2, 3)]

    late = pair // 8
    barrier = pltpu.get_barrier_semaphore()

    def signal(semaphore, virt_to, pair_to):
        pl.semaphore_signal(semaphore, inc=1, device_id={"virt": virt_to, "pair": pair_to}, device_id_type=MESH)

    @pl.when(late == 0)
    def _():
        for peer in far_peers:
            signal(barrier, peer, far_pair)

    for peer in [*x_peers, *cross_peers, *z_peers, partner]:
        signal(barrier, peer, pair)

    lane_tile = lax.broadcasted_iota(jnp.int32, (4, 384), 1) // TILE
    row_tile = lax.broadcasted_iota(jnp.int32, (4, 384), 0)
    spread = (lane_tile == row_tile).astype(F32)
    loads[0].wait()
    mask = lax.dot_general(
        mask_in[...].astype(F32), spread, (((0,), (0,)), ((), ())), preferred_element_type=F32
    )

    total = jnp.zeros((256, 384), F32)
    for i, (start, size) in enumerate(CHUNKS):
        loads[2 * i + 1].wait()
        loads[2 * i + 2].wait()
        if i == len(CHUNKS) - 1:
            pl.semaphore_wait(barrier, 10 + 4 * late)

            @pl.when(late == 1)
            def _():
                for peer in far_peers:
                    signal(ready, peer, far_pair)

        tiles = []
        for t in range(start // TILE, (start + size) // TILE):
            tiles.append(ints[t * TILE : (t + 1) * TILE, :] * mask[t : t + 1, :])
        b_high, b_low = split(jnp.concatenate(tiles, axis=0))
        a_high, a_low = split(amp[:, start : start + size])
        total += dot(a_high, b_high) + dot(a_high, b_low) + dot(a_low, b_high)
    left = total[:128].T
    right = total[128:].T
    sends = []

    def send(slot, src, dst, virt_to, pair_to):
        copy = pltpu.make_async_remote_copy(
            src_ref=src,
            dst_ref=dst,
            send_sem=send_sem.at[slot],
            recv_sem=recv_sem.at[slot],
            device_id={"virt": virt_to, "pair": pair_to},
            device_id_type=MESH,
        )
        copy.start()
        sends.append(copy)
        return copy

    halves = {}
    arrivals = {zb: [] for zb in range(4)}

    def pack(zb):
        for xb in range(4):
            for cc in (0, 1):
                first = 24 * (4 * xb + zb) + 12 * cc
                part[cc, zb, xb] = jnp.concatenate(
                    [left[first : first + 12], right[first : first + 12]], axis=0
                )

    pack(0)
    for dx in (2, 1, 3):
        column = (x + 2 + dx) % 4
        slot = dx - 1
        arrivals[0].append(
            send(4 + slot, part.at[core, 0, column], far_x_in.at[slot, 0], x_peers[slot], pair)
        )
        arrivals[0].append(
            send(35 + slot, part.at[other, 0, column], cross_in.at[slot], cross_peers[slot], pair)
        )
    for zb in (1, 2, 3, 0):
        if zb:
            pack(zb)
        halves[zb] = send(zb, part.at[other, zb], part_in.at[zb], partner, pair)

    loads[7].wait()
    rows = lax.broadcasted_iota(jnp.int32, (256, 256), 0)
    select[...] = (rows == mirror_row[...]).astype(F32).astype(BF16)

    for zb in (1, 2, 3, 0):
        halves[zb].wait_recv()
        summed[zb] = part[core, zb] + part_in[zb]
        if zb:
            for dx in (2, 1, 3):
                column = (x + 2 + dx) % 4
                slot = dx - 1
                arrivals[zb].append(
                    send(
                        4 + 3 * zb + slot,
                        summed.at[zb, column],
                        far_x_in.at[slot, zb],
                        x_peers[slot],
                        pair,
                    )
                )
    order = (0, 1, 2, 3)
    far = []
    for i, d in enumerate(order):
        far.append(
            pltpu.make_async_remote_copy(
                src_ref=far_x_sum.at[i],
                dst_ref=far_in.at[z],
                send_sem=send_sem.at[16 + i],
                recv_sem=recv_sem.at[16 + z],
                device_id={"virt": far_peers[d], "pair": far_pair},
                device_id_type=MESH,
            )
        )
    for i, d in enumerate(order):
        for copy in arrivals[d]:
            copy.wait_recv()
        kept = summed[d, (x + 2) % 4] + far_x_in[0, i] + far_x_in[1, i] + far_x_in[2, i]
        if d == 0:
            kept += cross_in[0] + cross_in[1] + cross_in[2]
        far_x_sum[i] = kept

        @pl.when(late == 1)
        def _(copy=far[i]):
            copy.start()

    own_order = (2, 1, 3, 0)
    arrivals = []
    for i, d in enumerate(own_order):
        for dx in (2, 1, 3):
            column = (x + dx) % 4
            arrivals.append(
                send(
                    20 + 3 * i + dx - 1,
                    summed.at[(z + d) % 4, column],
                    own_x_in.at[dx - 1, i],
                    x_peers[dx - 1],
                    pair,
                )
            )
    own_z = []
    for i, d in enumerate(own_order):
        for copy in arrivals[3 * i : 3 * i + 3]:
            copy.wait_recv()
        kept = summed[(z + d) % 4, x] + own_x_in[0, i] + own_x_in[1, i] + own_x_in[2, i]
        if d:
            own_x_sum[i] = kept
            own_z.append(send(32 + i, own_x_sum.at[i], own_z_in.at[i], z_peers[d - 1], pair))
    @pl.when(late == 0)
    def _():
        pl.semaphore_wait(ready, 4)
        for copy in far:
            copy.start()

    for copy in own_z:
        copy.wait_recv()
    own = unpack(kept + own_z_in[0] + own_z_in[1] + own_z_in[2])

    for copy in [*sends, *far]:
        copy.wait_send()

    for slot in range(4):
        pltpu.make_async_copy(far_in.at[slot], far_in.at[slot], recv_sem.at[16 + slot]).wait()
    turned = unpack(far_in[0] + far_in[1] + far_in[2] + far_in[3])
    turned = jnp.concatenate([turned, jnp.zeros((4, 256), F32)], axis=0)
    first = turned.astype(BF16)
    second, third = split(turned - first.astype(F32))
    moved = dot(jnp.concatenate([first, second, third], axis=0), select[...])
    out_ref[...] = own + (moved[0:12] + moved[16:28] + moved[32:44])


def shards(amplitudes, integrals, tile_mask, mirror_row):
    any_spec = pl.BlockSpec(memory_space=pl.ANY)
    result = pl.pallas_call(
        kernel,
        out_shape=pltpu.VMEM((12, 256), F32),
        in_specs=[any_spec] * 4,
        out_specs=pl.BlockSpec(memory_space=pltpu.VMEM),
        scratch_shapes=[
            pltpu.VMEM((256, 1920), F32),
            pltpu.VMEM((1920, 384), F32),
            pltpu.VMEM((4, 20), jnp.int32),
            pltpu.VMEM((1, 256), jnp.int32),
            pltpu.VMEM((2, 4, 4, 24, 128), F32),
            pltpu.VMEM((4, 4, 24, 128), F32),
            pltpu.VMEM((4, 4, 24, 128), F32),
            pltpu.VMEM((3, 4, 24, 128), F32),
            pltpu.VMEM((3, 24, 128), F32),
            pltpu.VMEM((4, 24, 128), F32),
            pltpu.VMEM((4, 24, 128), F32),
            pltpu.VMEM((3, 4, 24, 128), F32),
            pltpu.VMEM((3, 24, 128), F32),
            pltpu.VMEM((3, 24, 128), F32),
            pltpu.VMEM((256, 256), BF16),
            pltpu.SemaphoreType.DMA((8,)),
            pltpu.SemaphoreType.DMA((38,)),
            pltpu.SemaphoreType.DMA((38,)),
            pltpu.SemaphoreType.REGULAR,
        ],
        compiler_params=pltpu.CompilerParams(collective_id=0, has_side_effects=True),
        name="ladder",
    )(amplitudes, integrals, tile_mask.T, mirror_row.reshape(1, 256))
    return result.T


def solution(mesh):
    in_specs = (P("pair", "virt"), P("virt", None), P("virt", None), P("pair"))
    out_specs = P("pair", "virt")
    return jax.shard_map(shards, mesh=mesh, in_specs=in_specs, out_specs=out_specs, check_vma=False)
```

```python
import jax
import jax.numpy as jnp
from jax import lax
from jax.experimental import pallas as pl
from jax.experimental.pallas import tpu as pltpu
from jax.sharding import PartitionSpec as P

TILE = 96
CHUNKS = ((0, 256), (256, 512), (768, 768), (1536, 384))
F32 = jnp.float32
BF16 = jnp.bfloat16
MESH = pl.DeviceIdType.MESH


def split(value):
    high = value.astype(BF16)
    return high, (value - high.astype(F32)).astype(BF16)


def dot(left, right):
    return jnp.dot(left, right, preferred_element_type=F32)


def unpack(block):
    return jnp.concatenate([block[0:12], block[12:24]], axis=1)


def kernel(
    amp_hbm,
    int_hbm,
    mask_hbm,
    mirror_hbm,
    out_ref,
    amp,
    ints,
    mask_in,
    mirror_row,
    part,
    part_in,
    summed,
    far_x_in,
    cross_in,
    far_x_sum,
    far_in,
    own_x_in,
    own_x_sum,
    own_z_in,
    select,
    load_sem,
    send_sem,
    recv_sem,
    ready,
):
    loads = [pltpu.make_async_copy(mask_hbm, mask_in, load_sem.at[0])]
    for i, (start, size) in enumerate(CHUNKS):
        loads.append(
            pltpu.make_async_copy(
                int_hbm.at[pl.ds(start, size), :], ints.at[pl.ds(start, size), :], load_sem.at[2 * i + 1]
            )
        )
        loads.append(
            pltpu.make_async_copy(
                amp_hbm.at[:, pl.ds(start, size)], amp.at[:, pl.ds(start, size)], load_sem.at[2 * i + 2]
            )
        )
    loads.append(pltpu.make_async_copy(mirror_hbm, mirror_row, load_sem.at[9]))
    for i, load in enumerate(loads):
        load.start(priority=int(i > 2))

    virt = lax.axis_index("virt")
    pair = lax.axis_index("pair")
    core = virt % 2
    z = (virt // 2) % 4
    x = virt // 8
    other = 1 - core
    far_pair = (pair + 8) % 16

    def at(xx, zz, cc):
        return xx * 8 + zz * 2 + cc

    partner = at(x, z, other)
    x_peers = [at((x + d) % 4, z, core) for d in (1, 2, 3)]
    cross_peers = [at((x + d) % 4, z, other) for d in (1, 2, 3)]
    z_peers = [at(x, (z + d) % 4, core) for d in (1, 2, 3)]
    far_peers = [at(x, d, core) for d in (0, 1, 2, 3)]

    late = pair // 8
    barrier = pltpu.get_barrier_semaphore()

    def signal(semaphore, virt_to, pair_to):
        pl.semaphore_signal(semaphore, inc=1, device_id={"virt": virt_to, "pair": pair_to}, device_id_type=MESH)

    @pl.when(late == 0)
    def _():
        for peer in far_peers:
            signal(barrier, peer, far_pair)

    for peer in [*x_peers, *cross_peers, *z_peers, partner]:
        signal(barrier, peer, pair)

    lane_tile = lax.broadcasted_iota(jnp.int32, (4, 384), 1) // TILE
    row_tile = lax.broadcasted_iota(jnp.int32, (4, 384), 0)
    spread = (lane_tile == row_tile).astype(F32)
    loads[0].wait()
    mask = lax.dot_general(
        mask_in[...].astype(F32), spread, (((0,), (0,)), ((), ())), preferred_element_type=F32
    )

    total = jnp.zeros((256, 384), F32)
    for i, (start, size) in enumerate(CHUNKS):
        loads[2 * i + 1].wait()
        loads[2 * i + 2].wait()
        if i == len(CHUNKS) - 1:
            pl.semaphore_wait(barrier, 10 + 4 * late)

            @pl.when(late == 1)
            def _():
                for peer in far_peers:
                    signal(ready, peer, far_pair)

        tiles = []
        edges = sorted({start, start + size, *range(-(-start // TILE) * TILE, start + size, TILE)})
        for low, high in zip(edges, edges[1:]):
            t = low // TILE
            tiles.append(ints[low:high, :] * mask[t : t + 1, :])
        b_high, b_low = split(jnp.concatenate(tiles, axis=0))
        a_high, a_low = split(amp[:, start : start + size])
        both = dot(a_high, jnp.concatenate([b_high, b_low], axis=1))
        total += both[:, :384] + both[:, 384:] + dot(a_low, b_high)
    left = total[:128].T
    right = total[128:].T
    sends = []

    def send(slot, src, dst, virt_to, pair_to):
        copy = pltpu.make_async_remote_copy(
            src_ref=src,
            dst_ref=dst,
            send_sem=send_sem.at[slot],
            recv_sem=recv_sem.at[slot],
            device_id={"virt": virt_to, "pair": pair_to},
            device_id_type=MESH,
        )
        copy.start()
        sends.append(copy)
        return copy

    halves = {}
    arrivals = {zb: [] for zb in range(4)}

    def pack(zb):
        for xb in range(4):
            for cc in (0, 1):
                first = 24 * (4 * xb + zb) + 12 * cc
                part[cc, zb, xb] = jnp.concatenate(
                    [left[first : first + 12], right[first : first + 12]], axis=0
                )

    pack(0)
    for dx in (2, 1, 3):
        column = (x + 2 + dx) % 4
        slot = dx - 1
        arrivals[0].append(
            send(4 + slot, part.at[core, 0, column], far_x_in.at[slot, 0], x_peers[slot], pair)
        )
        arrivals[0].append(
            send(35 + slot, part.at[other, 0, column], cross_in.at[slot], cross_peers[slot], pair)
        )
    for zb in (1, 2, 3, 0):
        if zb:
            pack(zb)
        halves[zb] = send(zb, part.at[other, zb], part_in.at[zb], partner, pair)

    loads[9].wait()
    rows = lax.broadcasted_iota(jnp.int32, (256, 256), 0)
    select[...] = (rows == mirror_row[...]).astype(F32).astype(BF16)

    for zb in (1, 2, 3, 0):
        halves[zb].wait_recv()
        summed[zb] = part[core, zb] + part_in[zb]
        if zb:
            for dx in (2, 1, 3):
                column = (x + 2 + dx) % 4
                slot = dx - 1
                arrivals[zb].append(
                    send(
                        4 + 3 * zb + slot,
                        summed.at[zb, column],
                        far_x_in.at[slot, zb],
                        x_peers[slot],
                        pair,
                    )
                )
    order = (0, 1, 2, 3)
    far = []
    for i, d in enumerate(order):
        far.append(
            pltpu.make_async_remote_copy(
                src_ref=far_x_sum.at[i],
                dst_ref=far_in.at[z],
                send_sem=send_sem.at[16 + i],
                recv_sem=recv_sem.at[16 + z],
                device_id={"virt": far_peers[d], "pair": far_pair},
                device_id_type=MESH,
            )
        )
    for i, d in enumerate(order):
        for copy in arrivals[d]:
            copy.wait_recv()
        kept = summed[d, (x + 2) % 4] + far_x_in[0, i] + far_x_in[1, i] + far_x_in[2, i]
        if d == 0:
            kept += cross_in[0] + cross_in[1] + cross_in[2]
        far_x_sum[i] = kept

        @pl.when(late == 1)
        def _(copy=far[i]):
            copy.start()

    own_order = (2, 1, 3, 0)
    arrivals = []
    for i, d in enumerate(own_order):
        for dx in (2, 1, 3):
            column = (x + dx) % 4
            arrivals.append(
                send(
                    20 + 3 * i + dx - 1,
                    summed.at[(z + d) % 4, column],
                    own_x_in.at[dx - 1, i],
                    x_peers[dx - 1],
                    pair,
                )
            )
    own_z = []
    for i, d in enumerate(own_order):
        for copy in arrivals[3 * i : 3 * i + 3]:
            copy.wait_recv()
        kept = summed[(z + d) % 4, x] + own_x_in[0, i] + own_x_in[1, i] + own_x_in[2, i]
        if d:
            own_x_sum[i] = kept
            own_z.append(send(32 + i, own_x_sum.at[i], own_z_in.at[i], z_peers[d - 1], pair))
    @pl.when(late == 0)
    def _():
        pl.semaphore_wait(ready, 4)
        for copy in far:
            copy.start()

    for copy in own_z:
        copy.wait_recv()
    own = unpack(kept + own_z_in[0] + own_z_in[1] + own_z_in[2])

    for copy in [*sends, *far]:
        copy.wait_send()

    for slot in range(4):
        pltpu.make_async_copy(far_in.at[slot], far_in.at[slot], recv_sem.at[16 + slot]).wait()
    turned = unpack(far_in[0] + far_in[1] + far_in[2] + far_in[3])
    turned = jnp.concatenate([turned, jnp.zeros((4, 256), F32)], axis=0)
    first = turned.astype(BF16)
    second, third = split(turned - first.astype(F32))
    moved = dot(jnp.concatenate([first, second, third], axis=0), select[...])
    out_ref[...] = own + (moved[0:12] + moved[16:28] + moved[32:44])


def shards(amplitudes, integrals, tile_mask, mirror_row):
    any_spec = pl.BlockSpec(memory_space=pl.ANY)
    result = pl.pallas_call(
        kernel,
        out_shape=pltpu.VMEM((12, 256), F32),
        in_specs=[any_spec] * 4,
        out_specs=pl.BlockSpec(memory_space=pltpu.VMEM),
        scratch_shapes=[
            pltpu.VMEM((256, 1920), F32),
            pltpu.VMEM((1920, 384), F32),
            pltpu.VMEM((4, 20), jnp.int32),
            pltpu.VMEM((1, 256), jnp.int32),
            pltpu.VMEM((2, 4, 4, 24, 128), F32),
            pltpu.VMEM((4, 4, 24, 128), F32),
            pltpu.VMEM((4, 4, 24, 128), F32),
            pltpu.VMEM((3, 4, 24, 128), F32),
            pltpu.VMEM((3, 24, 128), F32),
            pltpu.VMEM((4, 24, 128), F32),
            pltpu.VMEM((4, 24, 128), F32),
            pltpu.VMEM((3, 4, 24, 128), F32),
            pltpu.VMEM((3, 24, 128), F32),
            pltpu.VMEM((3, 24, 128), F32),
            pltpu.VMEM((256, 256), BF16),
            pltpu.SemaphoreType.DMA((10,)),
            pltpu.SemaphoreType.DMA((38,)),
            pltpu.SemaphoreType.DMA((38,)),
            pltpu.SemaphoreType.REGULAR,
        ],
        compiler_params=pltpu.CompilerParams(collective_id=0, has_side_effects=True),
        name="ladder",
    )(amplitudes, integrals, tile_mask.T, mirror_row.reshape(1, 256))
    return result.T


def solution(mesh):
    in_specs = (P("pair", "virt"), P("virt", None), P("virt", None), P("pair"))
    out_specs = P("pair", "virt")
    return jax.shard_map(shards, mesh=mesh, in_specs=in_specs, out_specs=out_specs, check_vma=False)
```

```python
import jax
import jax.numpy as jnp
from jax import lax
from jax.experimental import pallas as pl
from jax.experimental.pallas import tpu as pltpu
from jax.sharding import PartitionSpec as P

TILE = 96
CHUNKS = ((0, 256), (256, 512), (768, 768), (1536, 384))
F32 = jnp.float32
BF16 = jnp.bfloat16
MESH = pl.DeviceIdType.MESH


def split(value):
    high = value.astype(BF16)
    return high, (value - high.astype(F32)).astype(BF16)


def dot(left, right):
    return jnp.dot(left, right, preferred_element_type=F32)


def unpack(block):
    return jnp.concatenate([block[0:12], block[12:24]], axis=1)


def kernel(
    amp_hbm,
    int_hbm,
    mask_hbm,
    mirror_hbm,
    out_ref,
    amp,
    ints,
    mask_in,
    mirror_row,
    part,
    part_in,
    summed,
    far_x_in,
    cross_in,
    straight_in,
    arrived,
    far_x_sum,
    far_in,
    own_x_in,
    own_x_sum,
    own_z_in,
    select,
    load_sem,
    send_sem,
    recv_sem,
    ready,
):
    loads = [pltpu.make_async_copy(mask_hbm, mask_in, load_sem.at[0])]
    for i, (start, size) in enumerate(CHUNKS):
        loads.append(
            pltpu.make_async_copy(
                int_hbm.at[pl.ds(start, size), :], ints.at[pl.ds(start, size), :], load_sem.at[2 * i + 1]
            )
        )
        loads.append(
            pltpu.make_async_copy(
                amp_hbm.at[:, pl.ds(start, size)], amp.at[:, pl.ds(start, size)], load_sem.at[2 * i + 2]
            )
        )
    loads.append(pltpu.make_async_copy(mirror_hbm, mirror_row, load_sem.at[9]))
    for i, load in enumerate(loads):
        load.start(priority=int(i > 2))

    virt = lax.axis_index("virt")
    pair = lax.axis_index("pair")
    core = virt % 2
    z = (virt // 2) % 4
    x = virt // 8
    other = 1 - core
    far_pair = (pair + 8) % 16

    def at(xx, zz, cc):
        return xx * 8 + zz * 2 + cc

    partner = at(x, z, other)
    x_peers = [at((x + d) % 4, z, core) for d in (1, 2, 3)]
    cross_peers = [at((x + d) % 4, z, other) for d in (1, 2, 3)]
    z_peers = [at(x, (z + d) % 4, core) for d in (1, 2, 3)]
    far_peers = [at(x, d, core) for d in (0, 1, 2, 3)]

    late = pair // 8
    even = 1 - (pair // 4) % 2
    straight = [even * (z == zb).astype(jnp.int32) for zb in range(4)]
    straight_peer = at((x + 2) % 4, z, core)
    barrier = pltpu.get_barrier_semaphore()

    def signal(semaphore, virt_to, pair_to):
        pl.semaphore_signal(semaphore, inc=1, device_id={"virt": virt_to, "pair": pair_to}, device_id_type=MESH)

    @pl.when(late == 0)
    def _():
        for peer in far_peers:
            signal(barrier, peer, far_pair)

        @pl.when(even == 1)
        def _():
            signal(barrier, straight_peer, far_pair)

    for peer in [*x_peers, *cross_peers, *z_peers, partner]:
        signal(barrier, peer, pair)

    lane_tile = lax.broadcasted_iota(jnp.int32, (4, 384), 1) // TILE
    row_tile = lax.broadcasted_iota(jnp.int32, (4, 384), 0)
    spread = (lane_tile == row_tile).astype(F32)
    loads[0].wait()
    mask = lax.dot_general(
        mask_in[...].astype(F32), spread, (((0,), (0,)), ((), ())), preferred_element_type=F32
    )

    total = jnp.zeros((256, 384), F32)
    for i, (start, size) in enumerate(CHUNKS):
        loads[2 * i + 1].wait()
        loads[2 * i + 2].wait()
        if i == len(CHUNKS) - 1:
            pl.semaphore_wait(barrier, 10 + (4 + even) * late)

            @pl.when(late == 1)
            def _():
                for peer in far_peers:
                    signal(ready, peer, far_pair)

                @pl.when(even == 1)
                def _():
                    signal(ready, straight_peer, far_pair)

        tiles = []
        edges = sorted({start, start + size, *range(-(-start // TILE) * TILE, start + size, TILE)})
        for low, high in zip(edges, edges[1:]):
            t = low // TILE
            tiles.append(ints[low:high, :] * mask[t : t + 1, :])
        b_high, b_low = split(jnp.concatenate(tiles, axis=0))
        a_high, a_low = split(amp[:, start : start + size])
        both = dot(a_high, jnp.concatenate([b_high, b_low], axis=1))
        total += both[:, :384] + both[:, 384:] + dot(a_low, b_high)
    left = total[:128].T
    right = total[128:].T
    sends = []

    def describe(slot, src, dst, virt_to, pair_to):
        return pltpu.make_async_remote_copy(
            src_ref=src,
            dst_ref=dst,
            send_sem=send_sem.at[slot],
            recv_sem=recv_sem.at[slot],
            device_id={"virt": virt_to, "pair": pair_to},
            device_id_type=MESH,
        )

    def send(*where):
        copy = describe(*where)
        copy.start()
        sends.append(copy)
        return copy

    halves = {}
    arrivals = {zb: [] for zb in range(4)}

    def pack(zb):
        for xb in range(4):
            for cc in (0, 1):
                first = 24 * (4 * xb + zb) + 12 * cc
                part[cc, zb, xb] = jnp.concatenate(
                    [left[first : first + 12], right[first : first + 12]], axis=0
                )

    def across(zb, dx, use_part):
        column = (x + 2 + dx) % 4
        slot = dx - 1
        src = part.at[core, zb, column] if use_part else summed.at[zb, column]
        copies = [describe(4 + 3 * zb + slot, src, far_x_in.at[slot, zb], x_peers[slot], pair)]
        if use_part:
            copies.append(
                describe(35 + slot, part.at[other, zb, column], cross_in.at[slot], cross_peers[slot], pair)
            )
        return copies

    long_x = {zb: across(zb, 2, zb == 0) for zb in range(4)}

    def start_long(zb):
        @pl.when(straight[zb] == 0)
        def _():
            for copy in long_x[zb]:
                copy.start()

    def start_short(zb):
        for dx in (1, 3):
            for copy in across(zb, dx, zb == 0):
                copy.start()
                sends.append(copy)
                arrivals[zb].append(copy)

    direct = describe(38, summed.at[z, x], straight_in, straight_peer, far_pair)

    pack(0)
    start_long(0)
    start_short(0)
    for zb in range(4):
        if zb:
            pack(zb)
        halves[zb] = send(zb, part.at[other, zb], part_in.at[zb], partner, pair)

    loads[9].wait()
    rows = lax.broadcasted_iota(jnp.int32, (256, 256), 0)
    select[...] = (rows == mirror_row[...]).astype(F32).astype(BF16)

    for zb in (0, 1, 2, 3):
        halves[zb].wait_recv()
        summed[zb] = part[core, zb] + part_in[zb]

        @pl.when(straight[zb] * late == 1)
        def _():
            direct.start()

        if zb:
            start_long(zb)
            start_short(zb)

    order = (0, 1, 2, 3)
    far = []
    for i, d in enumerate(order):
        far.append(
            pltpu.make_async_remote_copy(
                src_ref=far_x_sum.at[i],
                dst_ref=far_in.at[z],
                send_sem=send_sem.at[16 + i],
                recv_sem=recv_sem.at[16 + z],
                device_id={"virt": far_peers[d], "pair": far_pair},
                device_id_type=MESH,
            )
        )
    for i, d in enumerate(order):
        for copy in arrivals[d]:
            copy.wait_recv()
        kept = summed[d, (x + 2) % 4] + far_x_in[0, i] + far_x_in[2, i]
        if d == 0:
            kept += cross_in[0] + cross_in[2]
        far_x_sum[i] = kept

        @pl.when(straight[d] == 0)
        def _():
            for copy in long_x[d]:
                copy.wait_recv()
            more = far_x_in[1, d]
            if d == 0:
                more += cross_in[1]
            far_x_sum[d] += more

        @pl.when(late == 1)
        def _(copy=far[i]):
            copy.start()

    own_order = (2, 1, 3, 0)
    arrivals = []
    for i, d in enumerate(own_order):
        for dx in (2, 1, 3):
            column = (x + dx) % 4
            arrivals.append(
                send(
                    20 + 3 * i + dx - 1,
                    summed.at[(z + d) % 4, column],
                    own_x_in.at[dx - 1, i],
                    x_peers[dx - 1],
                    pair,
                )
            )
    own_z = []
    for i, d in enumerate(own_order):
        for copy in arrivals[3 * i : 3 * i + 3]:
            copy.wait_recv()
        kept = summed[(z + d) % 4, x] + own_x_in[0, i] + own_x_in[1, i] + own_x_in[2, i]
        if d:
            own_x_sum[i] = kept
            own_z.append(send(32 + i, own_x_sum.at[i], own_z_in.at[i], z_peers[d - 1], pair))
    @pl.when(late == 0)
    def _():
        pl.semaphore_wait(ready, 4 + even)
        for copy in far:
            copy.start()

        @pl.when(even == 1)
        def _():
            direct.start()

    for copy in own_z:
        copy.wait_recv()
    own = unpack(kept + own_z_in[0] + own_z_in[1] + own_z_in[2])

    for copy in [*sends, *far]:
        copy.wait_send()
    for zb in range(4):
        @pl.when(straight[zb] == 0)
        def _():
            for copy in long_x[zb]:
                copy.wait_send()


    for slot in range(4):
        pltpu.make_async_copy(far_in.at[slot], far_in.at[slot], recv_sem.at[16 + slot]).wait()
    arrived[...] = far_in[0] + far_in[1] + far_in[2] + far_in[3]

    @pl.when(even == 1)
    def _():
        direct.wait()
        arrived[...] += straight_in[...]

    turned = unpack(arrived[...])
    turned = jnp.concatenate([turned, jnp.zeros((4, 256), F32)], axis=0)
    first = turned.astype(BF16)
    second, third = split(turned - first.astype(F32))
    moved = dot(jnp.concatenate([first, second, third], axis=0), select[...])
    out_ref[...] = own + (moved[0:12] + moved[16:28] + moved[32:44])


def shards(amplitudes, integrals, tile_mask, mirror_row):
    any_spec = pl.BlockSpec(memory_space=pl.ANY)
    result = pl.pallas_call(
        kernel,
        out_shape=pltpu.VMEM((12, 256), F32),
        in_specs=[any_spec] * 4,
        out_specs=pl.BlockSpec(memory_space=pltpu.VMEM),
        scratch_shapes=[
            pltpu.VMEM((256, 1920), F32),
            pltpu.VMEM((1920, 384), F32),
            pltpu.VMEM((4, 20), jnp.int32),
            pltpu.VMEM((1, 256), jnp.int32),
            pltpu.VMEM((2, 4, 4, 24, 128), F32),
            pltpu.VMEM((4, 4, 24, 128), F32),
            pltpu.VMEM((4, 4, 24, 128), F32),
            pltpu.VMEM((3, 4, 24, 128), F32),
            pltpu.VMEM((3, 24, 128), F32),
            pltpu.VMEM((24, 128), F32),
            pltpu.VMEM((24, 128), F32),
            pltpu.VMEM((4, 24, 128), F32),
            pltpu.VMEM((4, 24, 128), F32),
            pltpu.VMEM((3, 4, 24, 128), F32),
            pltpu.VMEM((3, 24, 128), F32),
            pltpu.VMEM((3, 24, 128), F32),
            pltpu.VMEM((256, 256), BF16),
            pltpu.SemaphoreType.DMA((10,)),
            pltpu.SemaphoreType.DMA((39,)),
            pltpu.SemaphoreType.DMA((39,)),
            pltpu.SemaphoreType.REGULAR,
        ],
        compiler_params=pltpu.CompilerParams(collective_id=0, has_side_effects=True),
        name="ladder",
    )(amplitudes, integrals, tile_mask.T, mirror_row.reshape(1, 256))
    return result.T


def solution(mesh):
    in_specs = (P("pair", "virt"), P("virt", None), P("virt", None), P("pair"))
    out_specs = P("pair", "virt")
    return jax.shard_map(shards, mesh=mesh, in_specs=in_specs, out_specs=out_specs, check_vma=False)
```

```python
import jax
import jax.numpy as jnp
from jax import lax
from jax.experimental import pallas as pl
from jax.experimental.pallas import tpu as pltpu
from jax.sharding import PartitionSpec as P

TILE = 96
CHUNKS = ((0, 256), (256, 512), (768, 768), (1536, 384))
F32 = jnp.float32
BF16 = jnp.bfloat16
MESH = pl.DeviceIdType.MESH


def split(value):
    high = value.astype(BF16)
    return high, (value - high.astype(F32)).astype(BF16)


def dot(left, right):
    return jnp.dot(left, right, preferred_element_type=F32)


def unpack(block):
    return jnp.concatenate([block[0:12], block[12:24]], axis=1)


def kernel(
    amp_hbm,
    int_hbm,
    mask_hbm,
    mirror_hbm,
    out_ref,
    amp,
    ints,
    mask_in,
    mirror_row,
    part,
    part_in,
    summed,
    far_x_in,
    cross_in,
    straight_in,
    arrived,
    far_x_sum,
    far_in,
    own_x_in,
    own_x_sum,
    own_z_in,
    select,
    load_sem,
    send_sem,
    recv_sem,
    ready,
):
    loads = [pltpu.make_async_copy(mask_hbm, mask_in, load_sem.at[0])]
    for i, (start, size) in enumerate(CHUNKS):
        loads.append(
            pltpu.make_async_copy(
                int_hbm.at[pl.ds(start, size), :], ints.at[pl.ds(start, size), :], load_sem.at[2 * i + 1]
            )
        )
        loads.append(
            pltpu.make_async_copy(
                amp_hbm.at[:, pl.ds(start, size)], amp.at[:, pl.ds(start, size)], load_sem.at[2 * i + 2]
            )
        )
    loads.append(pltpu.make_async_copy(mirror_hbm, mirror_row, load_sem.at[9]))
    for i, load in enumerate(loads):
        load.start(priority=int(i > 2))

    virt = lax.axis_index("virt")
    pair = lax.axis_index("pair")
    core = virt % 2
    z = (virt // 2) % 4
    x = virt // 8
    other = 1 - core
    far_pair = (pair + 8) % 16

    def at(xx, zz, cc):
        return xx * 8 + zz * 2 + cc

    partner = at(x, z, other)
    x_peers = [at((x + d) % 4, z, core) for d in (1, 2, 3)]
    cross_peers = [at((x + d) % 4, z, other) for d in (1, 2, 3)]
    z_peers = [at(x, (z + d) % 4, core) for d in (1, 2, 3)]
    far_peers = [at(x, d, core) for d in (0, 1, 2, 3)]

    late = pair // 8
    even = 1 - (pair // 4) % 2
    straight = [even * (z == zb).astype(jnp.int32) for zb in range(4)]
    straight_peer = at((x + 2) % 4, z, core)
    barrier = pltpu.get_barrier_semaphore()

    def signal(semaphore, virt_to, pair_to):
        pl.semaphore_signal(semaphore, inc=1, device_id={"virt": virt_to, "pair": pair_to}, device_id_type=MESH)

    @pl.when(late == 0)
    def _():
        for peer in far_peers:
            signal(barrier, peer, far_pair)

        @pl.when(even == 1)
        def _():
            signal(barrier, straight_peer, far_pair)

    for peer in [*x_peers, *cross_peers, *z_peers, partner]:
        signal(barrier, peer, pair)

    lane_tile = lax.broadcasted_iota(jnp.int32, (4, 384), 1) // TILE
    row_tile = lax.broadcasted_iota(jnp.int32, (4, 384), 0)
    spread = (lane_tile == row_tile).astype(F32)
    loads[0].wait()
    mask = lax.dot_general(
        mask_in[...].astype(F32), spread, (((0,), (0,)), ((), ())), preferred_element_type=F32
    )

    total = jnp.zeros((256, 384), F32)
    for i, (start, size) in enumerate(CHUNKS):
        loads[2 * i + 1].wait()
        loads[2 * i + 2].wait()
        if i == len(CHUNKS) - 1:
            pl.semaphore_wait(barrier, 10 + (4 + even) * late)

        tiles = []
        edges = sorted({start, start + size, *range(-(-start // TILE) * TILE, start + size, TILE)})
        for low, high in zip(edges, edges[1:]):
            t = low // TILE
            tiles.append(ints[low:high, :] * mask[t : t + 1, :])
        b_high, b_low = split(jnp.concatenate(tiles, axis=0))
        a_high, a_low = split(amp[:, start : start + size])
        b_both = jnp.concatenate([b_high, b_low], axis=1)
        if i < len(CHUNKS) - 1:
            both = dot(a_high, b_both)
            total += both[:, :384] + both[:, 384:] + dot(a_low, b_high)
    sides = []
    for rows in (slice(0, 128), slice(128, 256)):
        both = dot(a_high[rows], b_both)
        sides.append((total[rows] + both[:, :384] + both[:, 384:] + dot(a_low[rows], b_high)).T)
    left, right = sides
    sends = []

    def describe(slot, src, dst, virt_to, pair_to):
        return pltpu.make_async_remote_copy(
            src_ref=src,
            dst_ref=dst,
            send_sem=send_sem.at[slot],
            recv_sem=recv_sem.at[slot],
            device_id={"virt": virt_to, "pair": pair_to},
            device_id_type=MESH,
        )

    def send(*where):
        copy = describe(*where)
        copy.start()
        sends.append(copy)
        return copy

    halves = {}
    arrivals = {zb: [] for zb in range(4)}

    def pack(zb):
        for xb in range(4):
            for cc in (0, 1):
                first = 24 * (4 * xb + zb) + 12 * cc
                part[cc, zb, xb] = jnp.concatenate(
                    [left[first : first + 12], right[first : first + 12]], axis=0
                )

    def across(zb, dx, use_part):
        column = (x + 2 + dx) % 4
        slot = dx - 1
        src = part.at[core, zb, column] if use_part else summed.at[zb, column]
        copies = [describe(4 + 3 * zb + slot, src, far_x_in.at[slot, zb], x_peers[slot], pair)]
        if use_part:
            copies.append(
                describe(35 + slot, part.at[other, zb, column], cross_in.at[slot], cross_peers[slot], pair)
            )
        return copies

    long_x = {zb: across(zb, 2, zb == 0) for zb in range(4)}

    def start_long(zb):
        @pl.when(straight[zb] == 0)
        def _():
            for copy in long_x[zb]:
                copy.start()

    def start_short(zb):
        for dx in (1, 3):
            for copy in across(zb, dx, zb == 0):
                copy.start()
                sends.append(copy)
                arrivals[zb].append(copy)

    direct = describe(38, summed.at[z, x], straight_in, straight_peer, far_pair)

    pack(0)
    start_long(0)
    start_short(0)
    for zb in (1, 0, 2, 3):
        if zb:
            pack(zb)
        halves[zb] = send(zb, part.at[other, zb], part_in.at[zb], partner, pair)

    @pl.when(late == 1)
    def _():
        for peer in far_peers:
            signal(ready, peer, far_pair)

        @pl.when(even == 1)
        def _():
            signal(ready, straight_peer, far_pair)

    loads[9].wait()
    rows = lax.broadcasted_iota(jnp.int32, (256, 256), 0)
    select[...] = (rows == mirror_row[...]).astype(F32).astype(BF16)

    for zb in (1, 0, 2, 3):
        halves[zb].wait_recv()
        summed[zb] = part[core, zb] + part_in[zb]

        @pl.when(straight[zb] * late == 1)
        def _():
            direct.start()

        if zb:
            start_long(zb)
            start_short(zb)

    order = (0, 1, 2, 3)
    far = []
    for i, d in enumerate(order):
        far.append(
            pltpu.make_async_remote_copy(
                src_ref=far_x_sum.at[i],
                dst_ref=far_in.at[z],
                send_sem=send_sem.at[16 + i],
                recv_sem=recv_sem.at[16 + z],
                device_id={"virt": far_peers[d], "pair": far_pair},
                device_id_type=MESH,
            )
        )
    for i, d in enumerate(order):
        for copy in arrivals[d]:
            copy.wait_recv()
        kept = summed[d, (x + 2) % 4] + far_x_in[0, i] + far_x_in[2, i]
        if d == 0:
            kept += cross_in[0] + cross_in[2]
        far_x_sum[i] = kept

        @pl.when(straight[d] == 0)
        def _():
            for copy in long_x[d]:
                copy.wait_recv()
            more = far_x_in[1, d]
            if d == 0:
                more += cross_in[1]
            far_x_sum[d] += more

        @pl.when(late == 1)
        def _(copy=far[i]):
            copy.start()

    own_order = (2, 1, 3, 0)
    arrivals = []
    for i, d in enumerate(own_order):
        for dx in (2, 1, 3):
            column = (x + dx) % 4
            arrivals.append(
                send(
                    20 + 3 * i + dx - 1,
                    summed.at[(z + d) % 4, column],
                    own_x_in.at[dx - 1, i],
                    x_peers[dx - 1],
                    pair,
                )
            )
    own_z = []
    for i, d in enumerate(own_order):
        for copy in arrivals[3 * i : 3 * i + 3]:
            copy.wait_recv()
        kept = summed[(z + d) % 4, x] + own_x_in[0, i] + own_x_in[1, i] + own_x_in[2, i]
        if d:
            own_x_sum[i] = kept
            own_z.append(send(32 + i, own_x_sum.at[i], own_z_in.at[i], z_peers[d - 1], pair))
    @pl.when(late == 0)
    def _():
        pl.semaphore_wait(ready, 4 + even)
        for copy in far:
            copy.start()

        @pl.when(even == 1)
        def _():
            direct.start()

    for copy in own_z:
        copy.wait_recv()
    own = unpack(kept + own_z_in[0] + own_z_in[1] + own_z_in[2])

    for copy in [*sends, *far]:
        copy.wait_send()
    for zb in range(4):
        @pl.when(straight[zb] == 0)
        def _():
            for copy in long_x[zb]:
                copy.wait_send()


    for slot in range(4):
        pltpu.make_async_copy(far_in.at[slot], far_in.at[slot], recv_sem.at[16 + slot]).wait()
    arrived[...] = far_in[0] + far_in[1] + far_in[2] + far_in[3]

    @pl.when(even == 1)
    def _():
        direct.wait()
        arrived[...] += straight_in[...]

    turned = unpack(arrived[...])
    turned = jnp.concatenate([turned, jnp.zeros((4, 256), F32)], axis=0)
    first = turned.astype(BF16)
    second, third = split(turned - first.astype(F32))
    moved = dot(jnp.concatenate([first, second, third], axis=0), select[...])
    out_ref[...] = own + (moved[0:12] + moved[16:28] + moved[32:44])


def shards(amplitudes, integrals, tile_mask, mirror_row):
    any_spec = pl.BlockSpec(memory_space=pl.ANY)
    result = pl.pallas_call(
        kernel,
        out_shape=pltpu.VMEM((12, 256), F32),
        in_specs=[any_spec] * 4,
        out_specs=pl.BlockSpec(memory_space=pltpu.VMEM),
        scratch_shapes=[
            pltpu.VMEM((256, 1920), F32),
            pltpu.VMEM((1920, 384), F32),
            pltpu.VMEM((4, 20), jnp.int32),
            pltpu.VMEM((1, 256), jnp.int32),
            pltpu.VMEM((2, 4, 4, 24, 128), F32),
            pltpu.VMEM((4, 4, 24, 128), F32),
            pltpu.VMEM((4, 4, 24, 128), F32),
            pltpu.VMEM((3, 4, 24, 128), F32),
            pltpu.VMEM((3, 24, 128), F32),
            pltpu.VMEM((24, 128), F32),
            pltpu.VMEM((24, 128), F32),
            pltpu.VMEM((4, 24, 128), F32),
            pltpu.VMEM((4, 24, 128), F32),
            pltpu.VMEM((3, 4, 24, 128), F32),
            pltpu.VMEM((3, 24, 128), F32),
            pltpu.VMEM((3, 24, 128), F32),
            pltpu.VMEM((256, 256), BF16),
            pltpu.SemaphoreType.DMA((10,)),
            pltpu.SemaphoreType.DMA((39,)),
            pltpu.SemaphoreType.DMA((39,)),
            pltpu.SemaphoreType.REGULAR,
        ],
        compiler_params=pltpu.CompilerParams(collective_id=0, has_side_effects=True),
        name="ladder",
    )(amplitudes, integrals, tile_mask.T, mirror_row.reshape(1, 256))
    return result.T


def solution(mesh):
    in_specs = (P("pair", "virt"), P("virt", None), P("virt", None), P("pair"))
    out_specs = P("pair", "virt")
    return jax.shard_map(shards, mesh=mesh, in_specs=in_specs, out_specs=out_specs, check_vma=False)
```

```python
import jax
import jax.numpy as jnp
from jax import lax
from jax.experimental import pallas as pl
from jax.experimental.pallas import tpu as pltpu
from jax.sharding import PartitionSpec as P

TILE = 96
CHUNKS = ((0, 256), (256, 512), (768, 768), (1536, 384))
F32 = jnp.float32
BF16 = jnp.bfloat16
MESH = pl.DeviceIdType.MESH


def split(value):
    high = value.astype(BF16)
    return high, (value - high.astype(F32)).astype(BF16)


def dot(left, right):
    return jnp.dot(left, right, preferred_element_type=F32)


def unpack(block):
    return jnp.concatenate([block[0:12], block[12:24]], axis=1)


def kernel(
    amp_hbm,
    int_hbm,
    mask_hbm,
    mirror_hbm,
    out_ref,
    amp,
    ints,
    mask_in,
    mirror_row,
    part,
    part_in,
    summed,
    far_x_in,
    cross_in,
    straight_in,
    arrived,
    far_x_sum,
    far_in,
    own_x_in,
    own_x_sum,
    own_z_in,
    select,
    load_sem,
    send_sem,
    recv_sem,
    ready,
):
    loads = [pltpu.make_async_copy(mask_hbm, mask_in, load_sem.at[0])]
    for i, (start, size) in enumerate(CHUNKS):
        loads.append(
            pltpu.make_async_copy(
                int_hbm.at[pl.ds(start, size), :], ints.at[pl.ds(start, size), :], load_sem.at[2 * i + 1]
            )
        )
        loads.append(
            pltpu.make_async_copy(
                amp_hbm.at[:, pl.ds(start, size)], amp.at[:, pl.ds(start, size)], load_sem.at[2 * i + 2]
            )
        )
    loads.append(pltpu.make_async_copy(mirror_hbm, mirror_row, load_sem.at[9]))
    for i, load in enumerate(loads):
        load.start(priority=int(i > 2))

    virt = lax.axis_index("virt")
    pair = lax.axis_index("pair")
    core = virt % 2
    z = (virt // 2) % 4
    x = virt // 8
    other = 1 - core
    far_pair = (pair + 8) % 16

    def at(xx, zz, cc):
        return xx * 8 + zz * 2 + cc

    partner = at(x, z, other)
    x_peers = [at((x + d) % 4, z, core) for d in (1, 2, 3)]
    cross_peers = [at((x + d) % 4, z, other) for d in (1, 2, 3)]
    z_peers = [at(x, (z + d) % 4, core) for d in (1, 2, 3)]
    far_peers = [at(x, d, core) for d in (0, 1, 2, 3)]

    late = pair // 8
    even = 1 - (pair // 4) % 2
    straight = [even * (z == zb).astype(jnp.int32) for zb in range(4)]
    straight_peer = at((x + 2) % 4, z, core)
    barrier = pltpu.get_barrier_semaphore()

    def signal(semaphore, virt_to, pair_to):
        pl.semaphore_signal(semaphore, inc=1, device_id={"virt": virt_to, "pair": pair_to}, device_id_type=MESH)

    @pl.when(late == 0)
    def _():
        for peer in far_peers:
            signal(barrier, peer, far_pair)

        @pl.when(even == 1)
        def _():
            signal(barrier, straight_peer, far_pair)

    for peer in [*x_peers, *cross_peers, *z_peers, partner]:
        signal(barrier, peer, pair)

    lane_tile = lax.broadcasted_iota(jnp.int32, (4, 384), 1) // TILE
    row_tile = lax.broadcasted_iota(jnp.int32, (4, 384), 0)
    spread = (lane_tile == row_tile).astype(F32)
    loads[0].wait()
    mask = lax.dot_general(
        mask_in[...].astype(F32), spread, (((0,), (0,)), ((), ())), preferred_element_type=F32
    )

    total = jnp.zeros((256, 384), F32)
    for i, (start, size) in enumerate(CHUNKS):
        loads[2 * i + 1].wait()
        loads[2 * i + 2].wait()
        if i == len(CHUNKS) - 1:
            pl.semaphore_wait(barrier, 10 + (4 + even) * late)

            @pl.when(late == 1)
            def _():
                for peer in far_peers:
                    signal(ready, peer, far_pair)

                @pl.when(even == 1)
                def _():
                    signal(ready, straight_peer, far_pair)

        tiles = []
        edges = sorted({start, start + size, *range(-(-start // TILE) * TILE, start + size, TILE)})
        for low, high in zip(edges, edges[1:]):
            t = low // TILE
            tiles.append(ints[low:high, :] * mask[t : t + 1, :])
        b_high, b_low = split(jnp.concatenate(tiles, axis=0))
        a_high, a_low = split(amp[:, start : start + size])
        both = dot(a_high, jnp.concatenate([b_high, b_low], axis=1))
        total += both[:, :384] + both[:, 384:] + dot(a_low, b_high)
    left = total[:128].T
    right = total[128:].T
    sends = []

    def describe(slot, src, dst, virt_to, pair_to):
        return pltpu.make_async_remote_copy(
            src_ref=src,
            dst_ref=dst,
            send_sem=send_sem.at[slot],
            recv_sem=recv_sem.at[slot],
            device_id={"virt": virt_to, "pair": pair_to},
            device_id_type=MESH,
        )

    def send(*where):
        copy = describe(*where)
        copy.start()
        sends.append(copy)
        return copy

    halves = {}
    arrivals = {zb: [] for zb in range(4)}

    def pack(zb):
        for xb in range(4):
            for cc in (0, 1):
                first = 24 * (4 * xb + zb) + 12 * cc
                part[cc, zb, xb] = jnp.concatenate(
                    [left[first : first + 12], right[first : first + 12]], axis=0
                )

    def across(zb, dx, use_part):
        column = (x + 2 + dx) % 4
        slot = dx - 1
        src = part.at[core, zb, column] if use_part else summed.at[zb, column]
        copies = [describe(4 + 3 * zb + slot, src, far_x_in.at[slot, zb], x_peers[slot], pair)]
        if use_part:
            copies.append(
                describe(35 + slot, part.at[other, zb, column], cross_in.at[slot], cross_peers[slot], pair)
            )
        return copies

    long_x = {zb: across(zb, 2, zb == 0) for zb in range(4)}

    def start_long(zb):
        @pl.when(straight[zb] == 0)
        def _():
            for copy in long_x[zb]:
                copy.start()

    def start_short(zb):
        for dx in (1, 3):
            for copy in across(zb, dx, zb == 0):
                copy.start()
                sends.append(copy)
                arrivals[zb].append(copy)

    direct = describe(38, summed.at[z, x], straight_in, straight_peer, far_pair)

    pack(0)
    start_long(0)
    start_short(0)
    for zb in (1, 0, 2, 3):
        if zb:
            pack(zb)
        halves[zb] = send(zb, part.at[other, zb], part_in.at[zb], partner, pair)

    loads[9].wait()
    rows = lax.broadcasted_iota(jnp.int32, (256, 256), 0)
    select[...] = (rows == mirror_row[...]).astype(F32).astype(BF16)

    for zb in (1, 0, 2, 3):
        halves[zb].wait_recv()
        summed[zb] = part[core, zb] + part_in[zb]

        @pl.when(straight[zb] * late == 1)
        def _():
            direct.start()

        if zb:
            start_long(zb)
            start_short(zb)

    order = (0, 1, 2, 3)
    far = []
    for i, d in enumerate(order):
        far.append(
            pltpu.make_async_remote_copy(
                src_ref=far_x_sum.at[i],
                dst_ref=far_in.at[z],
                send_sem=send_sem.at[16 + i],
                recv_sem=recv_sem.at[16 + z],
                device_id={"virt": far_peers[d], "pair": far_pair},
                device_id_type=MESH,
            )
        )
    for i, d in enumerate(order):
        for copy in arrivals[d]:
            copy.wait_recv()
        kept = summed[d, (x + 2) % 4] + far_x_in[0, i] + far_x_in[2, i]
        if d == 0:
            kept += cross_in[0] + cross_in[2]
        far_x_sum[i] = kept

        @pl.when(straight[d] == 0)
        def _():
            for copy in long_x[d]:
                copy.wait_recv()
            more = far_x_in[1, d]
            if d == 0:
                more += cross_in[1]
            far_x_sum[d] += more

        @pl.when(late == 1)
        def _(copy=far[i]):
            copy.start()

    own_order = (2, 1, 3, 0)
    arrivals = []
    for i, d in enumerate(own_order):
        for dx in (2, 1, 3):
            column = (x + dx) % 4
            arrivals.append(
                send(
                    20 + 3 * i + dx - 1,
                    summed.at[(z + d) % 4, column],
                    own_x_in.at[dx - 1, i],
                    x_peers[dx - 1],
                    pair,
                )
            )
    own_z = []
    for i, d in enumerate(own_order):
        for copy in arrivals[3 * i : 3 * i + 3]:
            copy.wait_recv()
        kept = summed[(z + d) % 4, x] + own_x_in[0, i] + own_x_in[1, i] + own_x_in[2, i]
        if d:
            own_x_sum[i] = kept
            own_z.append(send(32 + i, own_x_sum.at[i], own_z_in.at[i], z_peers[d - 1], pair))
    @pl.when(late == 0)
    def _():
        pl.semaphore_wait(ready, 4 + even)
        for copy in far:
            copy.start()

        @pl.when(even == 1)
        def _():
            direct.start()

    for copy in own_z:
        copy.wait_recv()
    own = unpack(kept + own_z_in[0] + own_z_in[1] + own_z_in[2])

    for copy in [*sends, *far]:
        copy.wait_send()
    for zb in range(4):
        @pl.when(straight[zb] == 0)
        def _():
            for copy in long_x[zb]:
                copy.wait_send()


    for slot in range(4):
        pltpu.make_async_copy(far_in.at[slot], far_in.at[slot], recv_sem.at[16 + slot]).wait()
    arrived[...] = far_in[0] + far_in[1] + far_in[2] + far_in[3]

    @pl.when(even == 1)
    def _():
        direct.wait()
        arrived[...] += straight_in[...]

    turned = unpack(arrived[...])
    turned = jnp.concatenate([turned, jnp.zeros((4, 256), F32)], axis=0)
    first = turned.astype(BF16)
    second, third = split(turned - first.astype(F32))
    moved = dot(jnp.concatenate([first, second, third], axis=0), select[...])
    out_ref[...] = own + (moved[0:12] + moved[16:28] + moved[32:44])


def shards(amplitudes, integrals, tile_mask, mirror_row):
    any_spec = pl.BlockSpec(memory_space=pl.ANY)
    result = pl.pallas_call(
        kernel,
        out_shape=pltpu.VMEM((12, 256), F32),
        in_specs=[any_spec] * 4,
        out_specs=pl.BlockSpec(memory_space=pltpu.VMEM),
        scratch_shapes=[
            pltpu.VMEM((256, 1920), F32),
            pltpu.VMEM((1920, 384), F32),
            pltpu.VMEM((4, 20), jnp.int32),
            pltpu.VMEM((1, 256), jnp.int32),
            pltpu.VMEM((2, 4, 4, 24, 128), F32),
            pltpu.VMEM((4, 4, 24, 128), F32),
            pltpu.VMEM((4, 4, 24, 128), F32),
            pltpu.VMEM((3, 4, 24, 128), F32),
            pltpu.VMEM((3, 24, 128), F32),
            pltpu.VMEM((24, 128), F32),
            pltpu.VMEM((24, 128), F32),
            pltpu.VMEM((4, 24, 128), F32),
            pltpu.VMEM((4, 24, 128), F32),
            pltpu.VMEM((3, 4, 24, 128), F32),
            pltpu.VMEM((3, 24, 128), F32),
            pltpu.VMEM((3, 24, 128), F32),
            pltpu.VMEM((256, 256), BF16),
            pltpu.SemaphoreType.DMA((10,)),
            pltpu.SemaphoreType.DMA((39,)),
            pltpu.SemaphoreType.DMA((39,)),
            pltpu.SemaphoreType.REGULAR,
        ],
        compiler_params=pltpu.CompilerParams(collective_id=0, has_side_effects=True),
        name="ladder",
    )(amplitudes, integrals, tile_mask.T, mirror_row.reshape(1, 256))
    return result.T


def solution(mesh):
    in_specs = (P("pair", "virt"), P("virt", None), P("virt", None), P("pair"))
    out_specs = P("pair", "virt")
    return jax.shard_map(shards, mesh=mesh, in_specs=in_specs, out_specs=out_specs, check_vma=False)
```
